32 devices in a mesh: group: 4 (over y, x), patch: 8 (over z, core).
Axes of the slice: x: 2, y: 2, z: 4, core: 2. Of those that a mesh axis runs over, the one named last changes fastest.
Arguments:
- node_tape: bfloat16 [4, 8192, 512], P('group', 'patch'), may hold values from -6 to 6
- edge_tape: bfloat16 [4, 8192, 512], P('group', 'patch'), may hold values from -6 to 6
- node_cot: bfloat16 [4, 8192, 512], P('group', 'patch'), may hold values from -6 to 6
- edge_cot: bfloat16 [4, 8192, 512], P('group', 'patch'), may hold values from -6 to 6
- w_edge_in: bfloat16 [1536, 512], replicated, may hold values from -0.15625 to 0.15625
- w_edge_out: bfloat16 [512, 512], replicated, may hold values from -0.25 to 0.25
- gain_edge: float32 [512], replicated, may hold values from 0.1 to 1.9
- w_node_in: bfloat16 [1024, 512], replicated, may hold values from -0.1875 to 0.1875
- w_node_out: bfloat16 [512, 512], replicated, may hold values from -0.25 to 0.25
- gain_node: float32 [512], replicated, may hold values from 0.1 to 1.9
- senders: int32 [64, 128], P('patch'), may hold values from 0 to 1279
- receivers: int32 [64, 128], P('patch'), may hold values from 0 to 1023
- tile_count: int32 [8], P('patch'), may hold values from 1 to 8, as said below
- send_rows: int32 [8, 256], P('patch'), may hold values from 0 to 1023
Outputs:
- edge_grad: bfloat16 [4, 8192, 512], P('group', 'patch')
- node_grad: bfloat16 [4, 8192, 512], P('group', 'patch')
- grad_edge_in: float32 [1536, 512], P('patch')
- grad_edge_out: float32 [512, 512], P('patch')
- grad_gain_edge: float32 [512], P('patch')
- grad_node_in: float32 [1024, 512], P('patch')
- grad_node_out: float32 [512, 512], P('patch')
- grad_gain_node: float32 [512], P('patch')
The draws below stay inside these ranges and needn't reach their ends.
Inputs may be any that keep to these rules, and one draw needn't show every extreme that they name: Tiles 0 to tile_count - 1 of a patch's 8 slots hold edges, the rest are padding; some patch has all 8 live. `senders`: A value s below 1024 is a node of the edge's own patch; 1024 + k is the k-th halo row that patch receives, rows p * 32 to (p + 1) * 32 - 1 coming from patch p. `receivers`: A node of the edge's own patch. `send_rows`: entry p * 32 + j of patch q's list is the own node whose latent is the j-th halo row patch p receives from q; every patch sends exactly 32 rows to every patch.
All inputs are finite; a program needn't handle non-finite values.
Results may differ from the reference program's by a relative error of at most 0.014.
Values may be sent and summed in bfloat16 or wider, within the bound.
A program may use at most 128 MiB of HBM per device.

```python
import jax
import jax.numpy as jnp
from jax import lax

L = 512
NODE_DEV = 1024
TCAP = 8
TILE = 128
HALO_DEV = 256
NODES = 8192
TILES = 64
EDGES = 8192
N_GROUP = 4
N_PATCH = 8


def draw_tile_count(key, part):
    devices = TILES // TCAP
    first_key, second_key, third_key = jax.random.split(jax.random.fold_in(key, 11), 3)
    lowest = jax.random.randint(first_key, (devices,), 1, TCAP // 2 + 1)
    crowded = jax.random.randint(second_key, (devices,), 0, 4) == 0
    chosen = jax.random.randint(third_key, (), 0, devices)
    filled = crowded | (jnp.arange(devices) == chosen)
    return jnp.where(filled, TCAP, lowest).astype(jnp.int32)


def set_ends(drawn, rng, smallest, top_value):
    longest = drawn.shape.index(max(drawn.shape))
    spots = []
    for shift in (0, 1):
        where = [jax.random.randint(jax.random.fold_in(rng, axis), (), 0, length) for axis, length in enumerate(drawn.shape)]
        where[longest] = (where[longest] + shift) % drawn.shape[longest]
        spots.append(tuple(where))
    return drawn.at[spots[0]].set(smallest).at[spots[1]].set(top_value)


def with_spikes(result, own_key, source, target, blocks, factor):
    def block_of(dim):
        return (jnp.arange(result.shape[dim]) // (result.shape[dim] // blocks)).reshape((-1,) + (1,) * (result.ndim - 1 - dim))

    first = jax.random.permutation(own_key, blocks)[block_of(target)]
    second = (block_of(target) + blocks // 2) % blocks
    return jnp.where((block_of(source) == first) | (block_of(source) == second), factor * result, result)


def block_levels(key, extent, cuts, least, largest):
    def one(position, shards_of):
        steps = jax.random.uniform(jax.random.fold_in(jax.random.fold_in(key, 6), position), (shards_of,), jnp.float32, least / len(cuts), largest / len(cuts))
        return jnp.repeat(jnp.exp(steps), extent[position] // shards_of).reshape((-1,) + (1,) * (len(extent) - position - 1))

    gain = one(*cuts[0])
    for cut in cuts[1:]:
        gain = gain * one(*cut)
    return gain


def bell_draw(key, shape, width, bound, cuts=(), kind=jnp.bfloat16):
    entries = jax.random.normal(key, shape, jnp.float32) * width
    if len(cuts) > 0:
        entries = block_levels(key, shape, cuts, -0.22, 0.18) * entries
    return jnp.clip(entries, min=-bound, max=bound).astype(kind)


def gaussian_with(own_key, extent, deviation, most, pieces, heavy, kind=jnp.bfloat16):
    values = deviation * jax.random.normal(own_key, extent, jnp.float32)
    if pieces:
        values = values * block_levels(own_key, extent, pieces, -0.22, 0.18)
    return jnp.clip(with_spikes(values, jax.random.fold_in(own_key, 3), *heavy), -most, most).astype(kind)


def setup_inputs(seed: int = 0) -> dict:
    arg_keys = jax.random.split(jax.random.key(seed), 15)
    node_tape = bell_draw(arg_keys[0], (N_GROUP, NODES, L), 1.0, 6.0, ((0, 4), (1, 8)))
    edge_tape = gaussian_with(arg_keys[1], (N_GROUP, EDGES, L), 1.0, 6.0, ((0, 4), (1, 8)), (1, 2, 8, 2.0))
    node_cot = bell_draw(arg_keys[2], (N_GROUP, NODES, L), 1.0, 6.0, ((0, 4), (1, 8)))
    edge_cot = bell_draw(arg_keys[3], (N_GROUP, EDGES, L), 1.0, 6.0, ((0, 4), (1, 8)))
    w_edge_in = bell_draw(arg_keys[4], (3 * L, L), (3 * L) ** -0.5, 0.15625)
    w_edge_out = bell_draw(arg_keys[5], (L, L), L ** -0.5, 0.25)
    gain_edge = jnp.clip(1.0 + 0.18 * jax.random.normal(arg_keys[6], (L,), jnp.float32), 0.1, 1.9)
    w_node_in = bell_draw(arg_keys[7], (2 * L, L), (2 * L) ** -0.5, 0.1875)
    w_node_out = bell_draw(arg_keys[8], (L, L), L ** -0.5, 0.25)
    gain_node = jnp.clip(1.0 + 0.18 * jax.random.normal(arg_keys[9], (L,), jnp.float32), 0.1, 1.9)
    senders = set_ends(jax.random.randint(arg_keys[10], (TILES, TILE), 0, NODE_DEV + HALO_DEV), jax.random.fold_in(arg_keys[10], 1), 0, (NODE_DEV + HALO_DEV) - 1).astype(jnp.int32)
    receivers = set_ends(jax.random.randint(arg_keys[11], (TILES, TILE), 0, NODE_DEV), jax.random.fold_in(arg_keys[11], 1), 0, NODE_DEV - 1).astype(jnp.int32)
    tile_count = draw_tile_count(jax.random.fold_in(arg_keys[14], 71), 0)
    send_rows = set_ends(jax.random.randint(arg_keys[13], (N_PATCH, HALO_DEV), 0, NODE_DEV), jax.random.fold_in(arg_keys[13], 1), 0, NODE_DEV - 1).astype(jnp.int32)
    return dict(node_tape=node_tape, edge_tape=edge_tape, node_cot=node_cot, edge_cot=edge_cot, w_edge_in=w_edge_in, w_edge_out=w_edge_out, gain_edge=gain_edge, w_node_in=w_node_in, w_node_out=w_node_out, gain_node=gain_node, senders=senders, receivers=receivers, tile_count=tile_count, send_rows=send_rows)


epsilon = 1e-05

def product(left, right):
    return jnp.dot(left, right, preferred_element_type=jnp.float32)

def silu_slope(values):
    squash = jax.nn.sigmoid(values)
    return squash * (1.0 + values * (1.0 - squash))

def normalize(values):
    centred = values - lax.optimization_barrier(jnp.mean(values, axis=1, keepdims=True))
    inverse = lax.rsqrt(lax.optimization_barrier(jnp.mean(centred * centred, axis=1, keepdims=True)) + epsilon)
    return (centred * inverse, inverse)

def normalize_back(upstream, normed, inverse):
    return inverse * (upstream - lax.optimization_barrier(jnp.mean(upstream, axis=1, keepdims=True)) - normed * lax.optimization_barrier(jnp.mean(upstream * normed, axis=1, keepdims=True)))

def member(node_rows, edge_rows, node_back, edge_back, weights, send_index, recv_index, live_mask):
    w_edge_in, w_edge_out, gain_edge, w_node_in, w_node_out, gain_node = weights
    features = node_rows.shape[1]
    node_count = node_rows.shape[0]
    edge_input = jnp.concatenate([edge_rows, node_rows[send_index], node_rows[recv_index]], axis=1)
    edge_first = product(edge_input, w_edge_in)
    hidden = jax.nn.silu(edge_first).astype(jnp.bfloat16)
    second = product(hidden, w_edge_out)
    normed_edge, inverse_edge = normalize(second)
    message = live_mask * (gain_edge.astype(jnp.float32) * normed_edge)
    gathered = jax.ops.segment_sum(message, recv_index, num_segments=node_count).astype(jnp.bfloat16)
    joined = jnp.concatenate([node_rows, gathered], axis=1)
    node_first = product(joined, w_node_in)
    node_hidden = jax.nn.silu(node_first).astype(jnp.bfloat16)
    node_second = product(node_hidden, w_node_out)
    normed_node, inverse_node = normalize(node_second)
    node_upstream = node_back.astype(jnp.float32)
    part_gain_node = lax.optimization_barrier(jnp.sum(node_upstream * normed_node, axis=0))
    grad_second = normalize_back(node_upstream * gain_node.astype(jnp.float32), normed_node, inverse_node).astype(jnp.bfloat16)
    part_node_out = product(node_hidden.T, grad_second)
    grad_first = (product(grad_second, w_node_out.T) * silu_slope(node_first)).astype(jnp.bfloat16)
    part_node_in = product(joined.T, grad_first)
    grad_joined = product(grad_first, w_node_in.T)
    grad_message = live_mask * (edge_back.astype(jnp.float32) + grad_joined[:, features:][recv_index])
    part_gain_edge = lax.optimization_barrier(jnp.sum(grad_message * normed_edge, axis=0))
    grad_edge_second = normalize_back(grad_message * gain_edge.astype(jnp.float32), normed_edge, inverse_edge).astype(jnp.bfloat16)
    part_edge_out = product(hidden.T, grad_edge_second)
    grad_edge_first = (product(grad_edge_second, w_edge_out.T) * silu_slope(edge_first)).astype(jnp.bfloat16)
    part_edge_in = product(edge_input.T, grad_edge_first)
    grad_input = product(grad_edge_first, w_edge_in.T)
    edge_grad = (live_mask * edge_back.astype(jnp.float32) + grad_input[:, :features]).astype(jnp.bfloat16)
    from_send = jax.ops.segment_sum(grad_input[:, features:2 * features], send_index, num_segments=node_count)
    from_recv = jax.ops.segment_sum(grad_input[:, 2 * features:], recv_index, num_segments=node_count)
    node_grad = (node_upstream + grad_joined[:, :features] + from_send + from_recv).astype(jnp.bfloat16)
    return (edge_grad, node_grad, (part_edge_in, part_edge_out, part_gain_edge, part_node_in, part_node_out, part_gain_node))

def reference(node_tape, edge_tape, node_cot, edge_cot, w_edge_in, w_edge_out, gain_edge, w_node_in, w_node_out, gain_node, senders, receivers, tile_count, send_rows):
    edge_slots = TCAP * TILE
    peer_rows = HALO_DEV // N_PATCH
    flat_send = senders.reshape(-1).astype(jnp.int32)
    slot_ids = jnp.arange(EDGES, dtype=jnp.int32)
    owner_dev = slot_ids // edge_slots
    halo_pos = jnp.maximum(flat_send - NODE_DEV, 0)
    source = halo_pos // peer_rows
    column = owner_dev * peer_rows + halo_pos % peer_rows
    remote = source * NODE_DEV + send_rows[source, column]
    send_index = jnp.where(flat_send < NODE_DEV, owner_dev * NODE_DEV + flat_send, remote).astype(jnp.int32)
    recv_index = (owner_dev * NODE_DEV + receivers.reshape(-1)).astype(jnp.int32)
    tile_slot = slot_ids % edge_slots // TILE
    live_mask = (tile_slot < tile_count[owner_dev]).astype(jnp.float32)[:, None]
    weights = (w_edge_in, w_edge_out, gain_edge, w_node_in, w_node_out, gain_node)

    def run_member(inputs):
        return member(inputs[0], inputs[1], inputs[2], inputs[3], weights, send_index, recv_index, live_mask)
    edge_grad, node_grad, partials = lax.map(run_member, (node_tape, edge_tape, node_cot, edge_cot))
    factor = (N_GROUP * EDGES) ** (-0.5)
    sums = [lax.optimization_barrier(jnp.sum(stack, axis=0)) * factor for stack in partials]
    return (edge_grad, node_grad, sums[0], sums[1], sums[2], sums[3], sums[4], sums[5])
```

```python
import functools

import jax
import jax.numpy as jnp
from jax import lax
from jax.experimental import pallas as pl
from jax.experimental.pallas import tpu as pltpu
from jax.sharding import PartitionSpec as P

epsilon = 1e-05
BF = jnp.bfloat16
F32 = jnp.float32
LANES = 128
PACK = 16
MESH = pl.DeviceIdType.MESH


def dot(left, right):
    return jnp.dot(left, right, preferred_element_type=F32)


def dot_rt(left, right):
    return lax.dot_general(left, right, (((1,), (1,)), ((), ())), preferred_element_type=F32)


def dot_lt(left, right):
    return lax.dot_general(left, right, (((0,), (0,)), ((), ())), preferred_element_type=F32)


def sigmoid(values):
    return 1.0 / (1.0 + jnp.exp(-values))


def silu_slope(values):
    squash = sigmoid(values)
    return squash * (1.0 + values * (1.0 - squash))


def normalize(values):
    centred = values - jnp.mean(values, axis=1, keepdims=True)
    inverse = lax.rsqrt(jnp.mean(centred * centred, axis=1, keepdims=True) + epsilon)
    return (centred * inverse, inverse)


def normalize_back(upstream, normed, inverse):
    return inverse * (
        upstream
        - jnp.mean(upstream, axis=1, keepdims=True)
        - normed * jnp.mean(upstream * normed, axis=1, keepdims=True)
    )


def hot(index, shape, axis, base):
    return jnp.where(lax.broadcasted_iota(jnp.int32, shape, axis) + base == index, 1.0, 0.0).astype(
        BF
    )


class Copies:
    def __init__(self, send_sems, recv_sems):
        self.send_sems, self.recv_sems, self.used = send_sems, recv_sems, 0

    def start(self, source, target, device):
        copy = pltpu.make_async_remote_copy(
            src_ref=source,
            dst_ref=target,
            send_sem=self.send_sems.at[self.used],
            recv_sem=self.recv_sems.at[self.used],
            device_id=device,
            device_id_type=MESH,
        )
        self.used += 1
        copy.start()
        return copy


def wait_all(copies):
    for copy in copies:
        copy.wait()


class Reduction:
    def __init__(self, copies, refs, depth, middle, place):
        self.copies, self.depth, self.middle = copies, depth, middle
        self.g, self.rc, self.a, self.r1x, self.r1y, self.b0, self.b1 = refs[:7]
        self.r2x, self.r2y, self.c, self.r3, self.f = refs[7:]
        self.gi, self.p, self.core, self.z, self.gx, self.gy, self.zs = place
        self.xpeer = {"group": self.gi + 1 - 2 * self.gx, "patch": self.p}
        self.ypeer = {"group": self.gi + 2 - 4 * self.gy, "patch": self.p}
        self.low = pl.ds(0, middle)
        self.high = pl.ds(middle, depth - middle)

    def step0(self):
        other = {"group": self.gi, "patch": self.p + 1 - 2 * self.core}
        self.wait = [self.copies.start(self.g.at[1 - self.core], self.rc, other)]

    def step1(self):
        wait_all(self.wait)

        @pl.loop(0, self.zs)
        def _(k):
            self.a[k] = (self.g[self.core, k].astype(F32) + self.rc[k].astype(F32)).astype(BF)

        self.wait = [
            self.copies.start(self.a.at[:, 1 - self.gx, :, self.low], self.r1x, self.xpeer),
            self.copies.start(self.a.at[:, :, 1 - self.gy, self.high], self.r1y, self.ypeer),
        ]

    def step2(self):
        wait_all(self.wait)

        @pl.loop(0, self.zs)
        def _(k):
            self.b0[k] = (
                self.a[k, self.gx, :, self.low].astype(F32) + self.r1x[k].astype(F32)
            ).astype(BF)
            self.b1[k] = (
                self.a[k, :, self.gy, self.high].astype(F32) + self.r1y[k].astype(F32)
            ).astype(BF)

        self.wait = [
            self.copies.start(self.b0.at[:, 1 - self.gy], self.r2y, self.ypeer),
            self.copies.start(self.b1.at[:, 1 - self.gx], self.r2x, self.xpeer),
        ]

    def step3(self):
        wait_all(self.wait)

        @pl.loop(0, self.zs)
        def _(k):
            self.c[k, self.low] = (
                self.b0[k, self.gy].astype(F32) + self.r2y[k].astype(F32)
            ).astype(BF)
            self.c[k, self.high] = (
                self.b1[k, self.gx].astype(F32) + self.r2x[k].astype(F32)
            ).astype(BF)

        self.wait = []
        for step in range(1, self.zs):
            there = lax.rem(self.z + step, self.zs)
            self.wait.append(
                self.copies.start(
                    self.c.at[there],
                    self.r3.at[step - 1],
                    {"group": self.gi, "patch": there * 2 + self.core},
                )
            )

    def step4(self):
        wait_all(self.wait)
        total = self.c[self.z].astype(F32)
        for step in range(1, self.zs):
            total += self.r3[step - 1].astype(F32)
        self.f[self.gx, self.gy] = total.astype(BF)
        low = self.f.at[self.gx, self.gy, self.low]
        high = self.f.at[self.gx, self.gy, self.high]
        self.wait = [
            self.copies.start(low, low, self.ypeer),
            self.copies.start(high, high, self.xpeer),
        ]

    def step5(self):
        wait_all(self.wait)
        low = self.f.at[self.gx, :, self.low]
        high = self.f.at[:, self.gy, self.high]
        self.wait = [
            self.copies.start(low, low, self.xpeer),
            self.copies.start(high, high, self.ypeer),
        ]

    def step6(self, outs, factor):
        wait_all(self.wait)
        for quarter in range(4):
            row = 0
            for out in outs:
                size = out.shape[0]
                out[:, quarter * LANES : (quarter + 1) * LANES] = (
                    self.f[quarter // 2, quarter % 2, row : row + size].astype(F32) * factor
                )
                row += size


def kernel(sizes, *refs):
    n_group, n_patch, padded, tile, tile_edges, fused, factor = sizes
    (
        node,
        edge,
        node_cot,
        edge_cot,
        w_ei,
        w_eo,
        gain_e,
        w_ni,
        w_no,
        gain_n,
        send_col,
        send_row,
        recv_col,
        recv_row,
        list_col,
        list_row,
        count,
    ) = refs[:17]
    edge_grad, node_grad, o_ei, o_eo, o_ni, o_no, o_gain = refs[17:24]
    (
        outgoing,
        incoming,
        spread,
        returned,
        x_s,
        x_r,
        e_first,
        hidden,
        normed,
        inverse,
        message,
        joined,
        n_hidden,
        g_second,
        g_first,
        acc,
        gj,
        ge_second,
        ge_first,
        gs,
        gr,
        gains,
        send_sems,
        recv_sems,
    ) = refs[24:48]
    nodes, width = node.shape
    edges = edge.shape[0]
    halo = n_patch * padded
    gi = lax.axis_index("group")
    p = lax.axis_index("patch")
    core = lax.rem(p, 2)
    z = lax.div(p, 2)
    gx = lax.rem(gi, 2)
    gy = lax.div(gi, 2)
    copies = Copies(send_sems, recv_sems)

    barrier = pltpu.get_barrier_semaphore()
    peers = [{"group": gi, "patch": lax.rem(p + d, n_patch)} for d in range(1, n_patch)]
    greeted = list(peers)
    if fused:
        greeted.append({"group": gi + 1 - 2 * gx, "patch": p})
        greeted.append({"group": gi + 2 - 4 * gy, "patch": p})
    for peer in greeted:
        pl.semaphore_signal(barrier, inc=1, device_id=peer, device_id_type=MESH)

    chosen = dot(hot(list_col[...], (halo, nodes), 1, 0), node[...]).astype(BF)
    outgoing[...] = chosen.reshape(n_patch, padded, width)
    pl.semaphore_wait(barrier, len(greeted))
    moving = [
        copies.start(outgoing.at[lax.rem(p + d, n_patch)], incoming.at[p], peers[d - 1])
        for d in range(1, n_patch)
    ]
    incoming[p] = outgoing[p]
    gains[...] = jnp.zeros_like(gains)

    def rows_of(k):
        return pl.ds(pl.multiple_of(k * tile, tile), tile)

    @pl.loop(0, edges // tile)
    def _(k):
        rows = rows_of(k)
        latent = dot(hot(recv_col[rows, :], (tile, nodes), 1, 0), node[...]).astype(BF)
        x_r[rows, :] = latent
        e_first[rows, :] = dot(edge[rows, :], w_ei[:width, :]) + dot(latent, w_ei[2 * width :, :])

    wait_all(moving)

    def live_of(k):
        slot = lax.broadcasted_iota(jnp.int32, (tile, 1), 0) + k * tile
        return jnp.where(slot < count[0] * tile_edges, 1.0, 0.0)

    @pl.loop(0, edges // tile)
    def _(k):
        rows = rows_of(k)
        index = send_col[rows, :]
        latent = dot(hot(index, (tile, nodes), 1, 0), node[...])
        latent += dot(hot(index, (tile, halo), 1, nodes), incoming[...].reshape(halo, width))
        latent = latent.astype(BF)
        x_s[rows, :] = latent
        first = e_first[rows, :] + dot(latent, w_ei[width : 2 * width, :])
        e_first[rows, :] = first
        hid = (first * sigmoid(first)).astype(BF)
        hidden[rows, :] = hid
        norm, inv = normalize(dot(hid, w_eo[...]))
        normed[rows, :] = norm
        inverse[rows, :] = inv
        message[rows, :] = (live_of(k) * (gain_e[...] * norm)).astype(BF)

    @pl.loop(0, nodes // tile)
    def _(k):
        rows = rows_of(k)
        got = dot(hot(recv_row[...], (tile, edges), 0, k * tile), message[...]).astype(BF)
        joined[rows, :] = got
        first = dot(node[rows, :], w_ni[:width, :]) + dot(got, w_ni[width:, :])
        hid = (first * sigmoid(first)).astype(BF)
        n_hidden[rows, :] = hid
        norm, inv = normalize(dot(hid, w_no[...]))
        up = node_cot[rows, :].astype(F32)
        gains[1:2, :] += jnp.sum(up * norm, axis=0, keepdims=True)
        second = normalize_back(up * gain_n[...], norm, inv).astype(BF)
        g_second[rows, :] = second
        grad = (dot_rt(second, w_no[...]) * silu_slope(first)).astype(BF)
        g_first[rows, :] = grad
        acc[rows, :] = up + dot_rt(grad, w_ni[:width, :])
        gj[rows, :] = dot_rt(grad, w_ni[width:, :]).astype(BF)

    if fused:
        red_n_refs, red_e_refs = refs[48:60], refs[60:72]
        zs = n_patch // 2
        place = (gi, p, core, z, gx, gy, zs)
        g_n, g_e = red_n_refs[0], red_e_refs[0]
        red_n = Reduction(copies, red_n_refs, g_n.shape[-2], red_n_refs[3].shape[-2], place)
        red_e = Reduction(copies, red_e_refs, g_e.shape[-2], red_e_refs[3].shape[-2], place)

        def put(target, k, row, size, value):
            value = value.astype(BF)
            for c in range(2):
                for quarter in range(4):
                    target[c, k, quarter // 2, quarter % 2, row : row + size, :] = value[
                        c * size : (c + 1) * size, quarter * LANES : (quarter + 1) * LANES
                    ]

        def terms(target, k, row, size, left, right, first=0):
            span = pl.ds(pl.multiple_of(k * 2 * size, LANES), 2 * size)
            put(target, k + first, row, size, dot_lt(left[:, span], right))

        d_ni, d_no = o_ni.shape[0], o_no.shape[0]
        d_ei, d_eo = o_ei.shape[0], o_eo.shape[0]
        half = zs // 2

        @pl.loop(0, half)
        def _(k):
            terms(g_n, k, 0, d_ni, node, g_first[...])
            terms(g_n, k, 0, d_ni, joined, g_first[...], half)

        @pl.loop(0, zs)
        def _(k):
            terms(g_n, k, d_ni, d_no, n_hidden, g_second[...])

        red_n.step0()
    else:
        o_ni[:width, :] = dot_lt(node[...], g_first[...])
        o_ni[width:, :] = dot_lt(joined[...], g_first[...])
        o_no[...] = dot_lt(n_hidden[...], g_second[...])

    def edge_back(k):
        rows = rows_of(k)
        taken = dot(hot(recv_col[rows, :], (tile, nodes), 1, 0), gj[...])
        live = live_of(k)
        norm = normed[rows, :]
        grad = live * (edge_cot[rows, :].astype(F32) + taken)
        gains[0:1, :] += jnp.sum(grad * norm, axis=0, keepdims=True)
        second = normalize_back(grad * gain_e[...], norm, inverse[rows, :]).astype(BF)
        ge_second[rows, :] = second
        ge_first[rows, :] = (
            dot_rt(second, w_eo[...]) * silu_slope(e_first[rows, :])
        ).astype(BF)

    count_tiles = edges // tile
    pl.loop(0, count_tiles // 2)(edge_back)
    if fused:
        red_n.step1()
    pl.loop(count_tiles // 2, count_tiles)(edge_back)

    if fused:
        red_n.step2()
        blocks = 2 * d_ei
        for k in range(zs):
            start, stop = k * blocks, (k + 1) * blocks
            parts = []
            for order, source in enumerate((edge, x_s, x_r)):
                lo = max(start, order * width) - order * width
                hi = min(stop, (order + 1) * width) - order * width
                if lo < hi:
                    parts.append(dot_lt(source[:, lo:hi], ge_first[...]))
            value = parts[0] if len(parts) == 1 else jnp.concatenate(parts, axis=0)
            put(g_e, k, 0, d_ei, value)

        @pl.loop(0, zs)
        def _(k):
            terms(g_e, k, d_ei, d_eo, hidden, ge_second[...])
            total = gains[...]
            put(g_e, k, d_ei + d_eo, PACK, jnp.concatenate([total, total], axis=0))

        red_e.step0()
        red_n.step3()
    else:
        o_ei[:width, :] = dot_lt(edge[...], ge_first[...])
        o_ei[width : 2 * width, :] = dot_lt(x_s[...], ge_first[...])
        o_ei[2 * width :, :] = dot_lt(x_r[...], ge_first[...])
        o_eo[...] = dot_lt(hidden[...], ge_second[...])
        o_gain[...] = gains[...]

    def input_back(k):
        rows = rows_of(k)
        grad = ge_first[rows, :]
        gs[rows, :] = dot_rt(grad, w_ei[width : 2 * width, :]).astype(BF)
        gr[rows, :] = dot_rt(grad, w_ei[2 * width :, :]).astype(BF)

    pl.loop(0, count_tiles)(input_back)
    sums = dot(hot(send_row[...], (halo, edges), 0, nodes), gs[...]).astype(BF)
    spread[...] = sums.reshape(n_patch, padded, width)
    moving = [
        copies.start(spread.at[lax.rem(p + d, n_patch)], returned.at[p], peers[d - 1])
        for d in range(1, n_patch)
    ]
    returned[p] = spread[p]
    if fused:
        red_e.step1()
        red_n.step4()

    @pl.loop(0, count_tiles)
    def _(k):
        rows = rows_of(k)
        edge_grad[rows, :] = (
            live_of(k) * edge_cot[rows, :].astype(F32) + dot_rt(ge_first[rows, :], w_ei[:width, :])
        ).astype(BF)

    if fused:
        red_e.step2()
        red_n.step5()

    def gather_back(k):
        rows = rows_of(k)
        acc[rows, :] += dot(hot(send_row[...], (tile, edges), 0, k * tile), gs[...]) + dot(
            hot(recv_row[...], (tile, edges), 0, k * tile), gr[...]
        )

    pl.loop(0, nodes // tile)(gather_back)
    if fused:
        red_e.step3()
        red_n.step6((o_ni, o_no), factor)
    wait_all(moving)

    @pl.loop(0, nodes // tile)
    def _(k):
        rows = rows_of(k)
        node_grad[rows, :] = (
            acc[rows, :]
            + dot(
                hot(list_row[...], (tile, halo), 0, k * tile),
                returned[...].reshape(halo, width),
            )
        ).astype(BF)

    if fused:
        red_e.step4()
        red_e.step5()
        red_e.step6((o_ei, o_eo, o_gain), factor)


def reduction_scratch(zs, depth, middle):
    rest = depth - middle
    shapes = (
        (2, zs, 2, 2, depth),
        (zs, 2, 2, depth),
        (zs, 2, 2, depth),
        (zs, 2, middle),
        (zs, 2, rest),
        (zs, 2, middle),
        (zs, 2, rest),
        (zs, rest),
        (zs, middle),
        (zs, depth),
        (zs - 1, depth),
        (2, 2, depth),
    )
    return [pltpu.VMEM(shape + (LANES,), BF) for shape in shapes]


def local(
    n_group,
    n_patch,
    node_tape,
    edge_tape,
    node_cot,
    edge_cot,
    w_edge_in,
    w_edge_out,
    gain_edge,
    w_node_in,
    w_node_out,
    gain_node,
    senders,
    receivers,
    tile_count,
    send_rows,
):
    nodes, width = node_tape.shape[1:]
    edges = edge_tape.shape[1]
    listed = send_rows.shape[1]
    peer_rows = listed // n_patch
    padded = -(-peer_rows // PACK) * PACK
    halo = n_patch * padded
    tile = min(2 * LANES, nodes, edges)
    factor = float(n_group * n_patch * edges) ** (-0.5)

    flat = senders.reshape(-1)
    beyond = flat - nodes
    if padded != peer_rows:
        beyond = beyond // peer_rows * padded + beyond % peer_rows
        flat = jnp.where(flat < nodes, flat, nodes + beyond)
    lists = jnp.pad(
        send_rows.reshape(n_patch, peer_rows), ((0, 0), (0, padded - peer_rows)), constant_values=-1
    )
    recv = receivers.reshape(-1)

    weights = (w_edge_in, w_edge_out, w_node_in, w_node_out)
    depths = [w.shape[0] // n_patch for w in weights]
    zs = n_patch // 2
    fused = (
        n_group == 4
        and n_patch % 4 == 0
        and width == 4 * LANES
        and all(d % PACK == 0 and 2 * d % LANES == 0 for d in depths)
    )
    scratch = [
        pltpu.VMEM((n_patch, padded, width), BF),
        pltpu.VMEM((n_patch, padded, width), BF),
        pltpu.VMEM((n_patch, padded, width), BF),
        pltpu.VMEM((n_patch, padded, width), BF),
        pltpu.VMEM((edges, width), BF),
        pltpu.VMEM((edges, width), BF),
        pltpu.VMEM((edges, width), F32),
        pltpu.VMEM((edges, width), BF),
        pltpu.VMEM((edges, width), F32),
        pltpu.VMEM((edges, 1), F32),
        pltpu.VMEM((edges, width), BF),
        pltpu.VMEM((nodes, width), BF),
        pltpu.VMEM((nodes, width), BF),
        pltpu.VMEM((nodes, width), BF),
        pltpu.VMEM((nodes, width), BF),
        pltpu.VMEM((nodes, width), F32),
        pltpu.VMEM((nodes, width), BF),
        pltpu.VMEM((edges, width), BF),
        pltpu.VMEM((edges, width), BF),
        pltpu.VMEM((edges, width), BF),
        pltpu.VMEM((edges, width), BF),
        pltpu.VMEM((PACK, width), F32),
    ]
    n_copies = 2 * (n_patch - 1)
    if fused:
        d_ei, d_eo, d_ni, d_no = depths
        depth_n = d_ni + d_no
        depth_e = d_ei + d_eo + PACK
        scratch_n = reduction_scratch(zs, depth_n, depth_n // 2 // PACK * PACK)
        scratch_e = reduction_scratch(zs, depth_e, -(-depth_e // 2 // PACK) * PACK)
        n_copies += 2 * (9 + zs - 1)
    else:
        d_ei, d_eo, d_ni, d_no = [w.shape[0] for w in weights]
        scratch_n, scratch_e = [], []
    scratch += [pltpu.SemaphoreType.DMA((n_copies,)), pltpu.SemaphoreType.DMA((n_copies,))]
    scratch += scratch_n + scratch_e

    vmem = pl.BlockSpec(memory_space=pltpu.VMEM)
    sizes = (n_group, n_patch, padded, tile, senders.shape[1], fused, factor)
    edge_grad, node_grad, p_ei, p_eo, p_ni, p_no, p_gain = pl.pallas_call(
        functools.partial(kernel, sizes),
        out_shape=[
            jax.ShapeDtypeStruct((edges, width), BF),
            jax.ShapeDtypeStruct((nodes, width), BF),
            jax.ShapeDtypeStruct((d_ei, width), F32),
            jax.ShapeDtypeStruct((d_eo, width), F32),
            jax.ShapeDtypeStruct((d_ni, width), F32),
            jax.ShapeDtypeStruct((d_no, width), F32),
            jax.ShapeDtypeStruct((PACK, width), F32),
        ],
        in_specs=[vmem] * 16 + [pl.BlockSpec(memory_space=pltpu.SMEM)],
        out_specs=[vmem] * 7,
        scratch_shapes=scratch,
        compiler_params=pltpu.CompilerParams(
            collective_id=0, has_side_effects=True, vmem_limit_bytes=63 * 1024 * 1024
        ),
    )(
        node_tape[0],
        edge_tape[0],
        node_cot[0],
        edge_cot[0],
        w_edge_in,
        w_edge_out,
        gain_edge[None],
        w_node_in,
        w_node_out,
        gain_node[None],
        flat[:, None],
        flat[None],
        recv[:, None],
        recv[None],
        lists.reshape(-1, 1),
        lists.reshape(1, -1),
        tile_count,
    )
    piece = width // n_patch
    if fused:
        own = lax.dynamic_slice(p_gain, (0, lax.axis_index("patch") * piece), (2, piece))
        return (edge_grad[None], node_grad[None], p_ei, p_eo, own[0], p_ni, p_no, own[1])

    def summed(value):
        part = lax.psum_scatter(value, "patch", scatter_dimension=0, tiled=True)
        return lax.psum(part.astype(BF), "group").astype(F32) * factor

    return (
        edge_grad[None],
        node_grad[None],
        summed(p_ei),
        summed(p_eo),
        summed(p_gain[0]),
        summed(p_ni),
        summed(p_no),
        summed(p_gain[1]),
    )


def solution(mesh):
    member = P("group", "patch", None)
    placed = (member,) * 4 + (P(),) * 6
    placed += (P("patch", None), P("patch", None), P("patch"), P("patch", None))
    rows = P("patch", None)
    return jax.shard_map(
        functools.partial(local, mesh.shape["group"], mesh.shape["patch"]),
        mesh=mesh,
        in_specs=placed,
        out_specs=(member, member, rows, rows, P("patch"), rows, rows, P("patch")),
        check_vma=False,
    )
```

```python
import functools

import jax
import jax.numpy as jnp
from jax import lax
from jax.experimental import pallas as pl
from jax.experimental.pallas import tpu as pltpu
from jax.sharding import PartitionSpec as P

epsilon = 1e-05
BF = jnp.bfloat16
F32 = jnp.float32
LANES = 128
PACK = 16
MESH = pl.DeviceIdType.MESH


def dot(left, right):
    return jnp.dot(left, right, preferred_element_type=F32)


def dot_rt(left, right):
    return lax.dot_general(left, right, (((1,), (1,)), ((), ())), preferred_element_type=F32)


def dot_lt(left, right):
    return lax.dot_general(left, right, (((0,), (0,)), ((), ())), preferred_element_type=F32)


def sigmoid(values):
    return 1.0 / (1.0 + jnp.exp(-values))


def silu_slope(values):
    squash = sigmoid(values)
    return squash * (1.0 + values * (1.0 - squash))


def normalize(values):
    centred = values - jnp.mean(values, axis=1, keepdims=True)
    inverse = lax.rsqrt(jnp.mean(centred * centred, axis=1, keepdims=True) + epsilon)
    return (centred * inverse, inverse)


def normalize_back(upstream, normed, inverse):
    return inverse * (
        upstream
        - jnp.mean(upstream, axis=1, keepdims=True)
        - normed * jnp.mean(upstream * normed, axis=1, keepdims=True)
    )


def hot(index, shape, axis, base):
    return jnp.where(lax.broadcasted_iota(jnp.int32, shape, axis) + base == index, 1.0, 0.0).astype(
        BF
    )


class Copies:
    def __init__(self, send_sems, recv_sems):
        self.send_sems, self.recv_sems, self.used = send_sems, recv_sems, 0

    def start(self, source, target, device):
        copy = pltpu.make_async_remote_copy(
            src_ref=source,
            dst_ref=target,
            send_sem=self.send_sems.at[self.used],
            recv_sem=self.recv_sems.at[self.used],
            device_id=device,
            device_id_type=MESH,
        )
        self.used += 1
        copy.start()
        return copy


def wait_all(copies):
    for copy in copies:
        copy.wait()


class Reduction:
    def __init__(self, copies, refs, depth, middle, place):
        self.copies, self.depth, self.middle = copies, depth, middle
        self.g, self.rc, self.a, self.r1x, self.r1y, self.b0, self.b1 = refs[:7]
        self.r2x, self.r2y, self.c, self.r3, self.f = refs[7:]
        self.gi, self.p, self.core, self.z, self.gx, self.gy, self.zs = place
        self.xpeer = {"group": self.gi + 1 - 2 * self.gx, "patch": self.p}
        self.ypeer = {"group": self.gi + 2 - 4 * self.gy, "patch": self.p}
        self.low = pl.ds(0, middle)
        self.high = pl.ds(middle, depth - middle)

    def step0(self):
        other = {"group": self.gi, "patch": self.p + 1 - 2 * self.core}
        self.wait = [self.copies.start(self.g.at[1 - self.core], self.rc, other)]

    def step1(self):
        wait_all(self.wait)

        @pl.loop(0, self.zs)
        def _(k):
            self.a[k] = (self.g[self.core, k].astype(F32) + self.rc[k].astype(F32)).astype(BF)

        self.wait = [
            self.copies.start(self.a.at[:, 1 - self.gx, :, self.low], self.r1x, self.xpeer),
            self.copies.start(self.a.at[:, :, 1 - self.gy, self.high], self.r1y, self.ypeer),
        ]

    def step2(self):
        wait_all(self.wait)

        @pl.loop(0, self.zs)
        def _(k):
            self.b0[k] = (
                self.a[k, self.gx, :, self.low].astype(F32) + self.r1x[k].astype(F32)
            ).astype(BF)
            self.b1[k] = (
                self.a[k, :, self.gy, self.high].astype(F32) + self.r1y[k].astype(F32)
            ).astype(BF)

        self.wait = [
            self.copies.start(self.b0.at[:, 1 - self.gy], self.r2y, self.ypeer),
            self.copies.start(self.b1.at[:, 1 - self.gx], self.r2x, self.xpeer),
        ]

    def step3(self):
        wait_all(self.wait)

        @pl.loop(0, self.zs)
        def _(k):
            self.c[k, self.low] = (
                self.b0[k, self.gy].astype(F32) + self.r2y[k].astype(F32)
            ).astype(BF)
            self.c[k, self.high] = (
                self.b1[k, self.gx].astype(F32) + self.r2x[k].astype(F32)
            ).astype(BF)

        self.wait = []
        for step in range(1, self.zs):
            there = lax.rem(self.z + step, self.zs)
            self.wait.append(
                self.copies.start(
                    self.c.at[there],
                    self.r3.at[step - 1],
                    {"group": self.gi, "patch": there * 2 + self.core},
                )
            )

    def step4(self):
        wait_all(self.wait)
        total = self.c[self.z].astype(F32)
        for step in range(1, self.zs):
            total += self.r3[step - 1].astype(F32)
        self.f[self.gx, self.gy] = total.astype(BF)
        low = self.f.at[self.gx, self.gy, self.low]
        high = self.f.at[self.gx, self.gy, self.high]
        self.wait = [
            self.copies.start(low, low, self.ypeer),
            self.copies.start(high, high, self.xpeer),
        ]

    def step5(self):
        wait_all(self.wait)
        low = self.f.at[self.gx, :, self.low]
        high = self.f.at[:, self.gy, self.high]
        self.wait = [
            self.copies.start(low, low, self.xpeer),
            self.copies.start(high, high, self.ypeer),
        ]

    def step6(self, outs, factor):
        wait_all(self.wait)
        for quarter in range(4):
            row = 0
            for out in outs:
                size = out.shape[0]
                out[:, quarter * LANES : (quarter + 1) * LANES] = (
                    self.f[quarter // 2, quarter % 2, row : row + size].astype(F32) * factor
                )
                row += size


def kernel(sizes, *refs):
    n_group, n_patch, padded, tile, tile_edges, fused, factor = sizes
    stored = refs[:8]
    gain_e, gain_n, send_tiles, recv_tiles, list_tiles, count = refs[8:14]
    edge_out, node_out, o_ei, o_eo, o_ni, o_no, o_gain = refs[14:21]
    loaded = refs[21:29]
    node, edge, w_ei, w_eo, w_ni, w_no, node_cot, edge_cot = loaded
    edge_grad, node_grad, load_sems, store_sems = refs[29:33]
    send_col, send_row, recv_col, recv_row, list_col, list_row = refs[33:39]
    refs = refs[15:]
    (
        outgoing,
        incoming,
        spread,
        returned,
        x_s,
        x_r,
        e_first,
        hidden,
        normed,
        inverse,
        message,
        joined,
        n_hidden,
        g_second,
        g_first,
        acc,
        gj,
        ge_second,
        ge_first,
        gs,
        gr,
        gains,
        send_sems,
        recv_sems,
    ) = refs[24:48]
    nodes, width = node.shape
    edges = edge.shape[0]
    halo = n_patch * padded
    gi = lax.axis_index("group")
    p = lax.axis_index("patch")
    core = lax.rem(p, 2)
    z = lax.div(p, 2)
    gx = lax.rem(gi, 2)
    gy = lax.div(gi, 2)
    copies = Copies(send_sems, recv_sems)
    loads = [
        pltpu.make_async_copy(source, target, load_sems.at[order])
        for order, (source, target) in enumerate(zip(stored, loaded))
    ]
    for load in loads:
        load.start()

    barrier = pltpu.get_barrier_semaphore()
    peers = [{"group": gi, "patch": lax.rem(p + d, n_patch)} for d in range(1, n_patch)]
    greeted = list(peers)
    if fused:
        greeted.append({"group": gi + 1 - 2 * gx, "patch": p})
        greeted.append({"group": gi + 2 - 4 * gy, "patch": p})
    for peer in greeted:
        pl.semaphore_signal(barrier, inc=1, device_id=peer, device_id_type=MESH)

    for tiles, column, line in (
        (list_tiles, list_col, list_row),
        (send_tiles, send_col, send_row),
        (recv_tiles, recv_col, recv_row),
    ):
        turned = jnp.transpose(tiles[...].astype(F32)).astype(jnp.int32)
        for order in range(line.shape[1] // LANES):
            span = slice(order * LANES, (order + 1) * LANES)
            column[span, :] = turned[:, order : order + 1]
            line[:, span] = tiles[order : order + 1, :]

    loads[0].wait()
    chosen = dot(hot(list_col[...], (halo, nodes), 1, 0), node[...]).astype(BF)
    outgoing[...] = chosen.reshape(n_patch, padded, width)
    pl.semaphore_wait(barrier, len(greeted))
    moving = [
        copies.start(outgoing.at[lax.rem(p + d, n_patch)], incoming.at[p], peers[d - 1])
        for d in range(1, n_patch)
    ]
    incoming[p] = outgoing[p]
    gains[...] = jnp.zeros_like(gains)

    loads[1].wait()
    loads[2].wait()

    def rows_of(k):
        return pl.ds(pl.multiple_of(k * tile, tile), tile)

    @pl.loop(0, edges // tile)
    def _(k):
        rows = rows_of(k)
        latent = dot(hot(recv_col[rows, :], (tile, nodes), 1, 0), node[...]).astype(BF)
        x_r[rows, :] = latent
        e_first[rows, :] = dot(edge[rows, :], w_ei[:width, :]) + dot(latent, w_ei[2 * width :, :])

    loads[3].wait()
    wait_all(moving)

    def live_of(k):
        slot = lax.broadcasted_iota(jnp.int32, (tile, 1), 0) + k * tile
        return jnp.where(slot < count[0] * tile_edges, 1.0, 0.0)

    @pl.loop(0, edges // tile)
    def _(k):
        rows = rows_of(k)
        index = send_col[rows, :]
        latent = dot(hot(index, (tile, nodes), 1, 0), node[...])
        latent += dot(hot(index, (tile, halo), 1, nodes), incoming[...].reshape(halo, width))
        latent = latent.astype(BF)
        x_s[rows, :] = latent
        first = e_first[rows, :] + dot(latent, w_ei[width : 2 * width, :])
        e_first[rows, :] = first
        hid = (first * sigmoid(first)).astype(BF)
        hidden[rows, :] = hid
        norm, inv = normalize(dot(hid, w_eo[...]))
        normed[rows, :] = norm
        inverse[rows, :] = inv
        message[rows, :] = (live_of(k) * (gain_e[...] * norm)).astype(BF)

    for load in loads[4:]:
        load.wait()

    @pl.loop(0, nodes // tile)
    def _(k):
        rows = rows_of(k)
        got = dot(hot(recv_row[...], (tile, edges), 0, k * tile), message[...]).astype(BF)
        joined[rows, :] = got
        first = dot(node[rows, :], w_ni[:width, :]) + dot(got, w_ni[width:, :])
        hid = (first * sigmoid(first)).astype(BF)
        n_hidden[rows, :] = hid
        norm, inv = normalize(dot(hid, w_no[...]))
        up = node_cot[rows, :].astype(F32)
        gains[1:2, :] += jnp.sum(up * norm, axis=0, keepdims=True)
        second = normalize_back(up * gain_n[...], norm, inv).astype(BF)
        g_second[rows, :] = second
        grad = (dot_rt(second, w_no[...]) * silu_slope(first)).astype(BF)
        g_first[rows, :] = grad
        acc[rows, :] = up + dot_rt(grad, w_ni[:width, :])
        gj[rows, :] = dot_rt(grad, w_ni[width:, :]).astype(BF)

    if fused:
        red_n_refs, red_e_refs, red_o_refs = refs[48:60], refs[60:72], refs[72:84]
        zs = n_patch // 2
        place = (gi, p, core, z, gx, gy, zs)
        g_n, g_e, g_o = red_n_refs[0], red_e_refs[0], red_o_refs[0]
        red_n = Reduction(copies, red_n_refs, g_n.shape[-2], red_n_refs[3].shape[-2], place)
        red_e = Reduction(copies, red_e_refs, g_e.shape[-2], red_e_refs[3].shape[-2], place)
        red_o = Reduction(copies, red_o_refs, g_o.shape[-2], red_o_refs[3].shape[-2], place)

        def put(target, k, row, size, value):
            value = value.astype(BF)
            for c in range(2):
                for quarter in range(4):
                    target[c, k, quarter // 2, quarter % 2, row : row + size, :] = value[
                        c * size : (c + 1) * size, quarter * LANES : (quarter + 1) * LANES
                    ]

        def terms(target, k, row, size, left, right, first=0):
            span = pl.ds(pl.multiple_of(k * 2 * size, LANES), 2 * size)
            put(target, k + first, row, size, dot_lt(left[:, span], right))

        d_ni, d_no = o_ni.shape[0], o_no.shape[0]
        d_ei, d_eo = o_ei.shape[0], o_eo.shape[0]
        half = zs // 2

        @pl.loop(0, half)
        def _(k):
            terms(g_n, k, 0, d_ni, node, g_first[...])
            terms(g_n, k, 0, d_ni, joined, g_first[...], half)

        @pl.loop(0, zs)
        def _(k):
            terms(g_n, k, d_ni, d_no, n_hidden, g_second[...])

        red_n.step0()
    else:
        o_ni[:width, :] = dot_lt(node[...], g_first[...])
        o_ni[width:, :] = dot_lt(joined[...], g_first[...])
        o_no[...] = dot_lt(n_hidden[...], g_second[...])

    def edge_back(k):
        rows = rows_of(k)
        taken = dot(hot(recv_col[rows, :], (tile, nodes), 1, 0), gj[...])
        live = live_of(k)
        norm = normed[rows, :]
        grad = live * (edge_cot[rows, :].astype(F32) + taken)
        gains[0:1, :] += jnp.sum(grad * norm, axis=0, keepdims=True)
        second = normalize_back(grad * gain_e[...], norm, inverse[rows, :]).astype(BF)
        ge_second[rows, :] = second
        ge_first[rows, :] = (
            dot_rt(second, w_eo[...]) * silu_slope(e_first[rows, :])
        ).astype(BF)

    count_tiles = edges // tile
    pl.loop(0, count_tiles)(edge_back)

    if fused:
        red_n.step1()
        blocks = 2 * d_ei
        for k in range(zs):
            start, stop = k * blocks, (k + 1) * blocks
            parts = []
            for order, source in enumerate((edge, x_s, x_r)):
                lo = max(start, order * width) - order * width
                hi = min(stop, (order + 1) * width) - order * width
                if lo < hi:
                    parts.append(dot_lt(source[:, lo:hi], ge_first[...]))
            value = parts[0] if len(parts) == 1 else jnp.concatenate(parts, axis=0)
            put(g_e, k, 0, d_ei, value)

        red_e.step0()
        red_n.step2()

        @pl.loop(0, zs)
        def _(k):
            terms(g_o, k, 0, d_eo, hidden, ge_second[...])
            total = gains[...]
            put(g_o, k, d_eo, PACK, jnp.concatenate([total, total], axis=0))

        red_o.step0()
    else:
        o_ei[:width, :] = dot_lt(edge[...], ge_first[...])
        o_ei[width : 2 * width, :] = dot_lt(x_s[...], ge_first[...])
        o_ei[2 * width :, :] = dot_lt(x_r[...], ge_first[...])
        o_eo[...] = dot_lt(hidden[...], ge_second[...])
        o_gain[...] = gains[...]

    def input_back(k):
        rows = rows_of(k)
        grad = ge_first[rows, :]
        gs[rows, :] = dot_rt(grad, w_ei[width : 2 * width, :]).astype(BF)
        gr[rows, :] = dot_rt(grad, w_ei[2 * width :, :]).astype(BF)

    pl.loop(0, count_tiles)(input_back)
    sums = dot(hot(send_row[...], (halo, edges), 0, nodes), gs[...]).astype(BF)
    spread[...] = sums.reshape(n_patch, padded, width)
    moving = [
        copies.start(spread.at[lax.rem(p + d, n_patch)], returned.at[p], peers[d - 1])
        for d in range(1, n_patch)
    ]
    returned[p] = spread[p]
    if fused:
        red_e.step1()
        red_n.step3()

    @pl.loop(0, count_tiles)
    def _(k):
        rows = rows_of(k)
        edge_grad[rows, :] = (
            live_of(k) * edge_cot[rows, :].astype(F32) + dot_rt(ge_first[rows, :], w_ei[:width, :])
        ).astype(BF)

    stores = [pltpu.make_async_copy(edge_grad, edge_out, store_sems.at[0])]
    stores[0].start()
    if fused:
        red_o.step1()
        red_n.step4()

    def gather_back(k):
        rows = rows_of(k)
        acc[rows, :] += dot(hot(send_row[...], (tile, edges), 0, k * tile), gs[...]) + dot(
            hot(recv_row[...], (tile, edges), 0, k * tile), gr[...]
        )

    middle = nodes // tile // 2
    pl.loop(0, middle)(gather_back)
    if fused:
        red_e.step2()
        red_o.step2()
        red_n.step5()
    pl.loop(middle, nodes // tile)(gather_back)
    if fused:
        red_e.step3()
        red_o.step3()
        red_n.step6((o_ni, o_no), factor)
    wait_all(moving)

    @pl.loop(0, nodes // tile)
    def _(k):
        rows = rows_of(k)
        node_grad[rows, :] = (
            acc[rows, :]
            + dot(
                hot(list_row[...], (tile, halo), 0, k * tile),
                returned[...].reshape(halo, width),
            )
        ).astype(BF)

    stores.append(pltpu.make_async_copy(node_grad, node_out, store_sems.at[1]))
    stores[1].start()
    if fused:
        red_e.step4()
        red_o.step4()
        red_e.step5()
        red_o.step5()
        red_e.step6((o_ei,), factor)
        red_o.step6((o_eo,), factor)
        piece = o_gain.shape[1]
        own = jnp.zeros(o_gain.shape, F32)
        for quarter in range(4):
            lane = lax.broadcasted_iota(jnp.int32, (LANES, piece), 0) + quarter * LANES
            want = lax.broadcasted_iota(jnp.int32, (LANES, piece), 1) + p * piece
            pick = jnp.where(lane == want, 1.0, 0.0).astype(BF)
            own += dot(red_o.f[quarter // 2, quarter % 2, d_eo : d_eo + PACK], pick)
        o_gain[...] = own * factor
    for store in stores:
        store.wait()


def reduction_scratch(zs, depth, middle):
    rest = depth - middle
    shapes = (
        (2, zs, 2, 2, depth),
        (zs, 2, 2, depth),
        (zs, 2, 2, depth),
        (zs, 2, middle),
        (zs, 2, rest),
        (zs, 2, middle),
        (zs, 2, rest),
        (zs, rest),
        (zs, middle),
        (zs, depth),
        (zs - 1, depth),
        (2, 2, depth),
    )
    return [pltpu.VMEM(shape + (LANES,), BF) for shape in shapes]


def tiles_of(index):
    rows = -(-index.shape[0] // LANES)
    full = -(-rows // 8) * 8
    return jnp.pad(index, (0, full * LANES - index.shape[0])).reshape(full, LANES)


def local(
    n_group,
    n_patch,
    node_tape,
    edge_tape,
    node_cot,
    edge_cot,
    w_edge_in,
    w_edge_out,
    gain_edge,
    w_node_in,
    w_node_out,
    gain_node,
    senders,
    receivers,
    tile_count,
    send_rows,
):
    nodes, width = node_tape.shape[1:]
    edges = edge_tape.shape[1]
    listed = send_rows.shape[1]
    peer_rows = listed // n_patch
    padded = -(-peer_rows // PACK) * PACK
    halo = n_patch * padded
    tile = min(2 * LANES, nodes, edges)
    factor = float(n_group * n_patch * edges) ** (-0.5)

    flat = senders.reshape(-1)
    beyond = flat - nodes
    if padded != peer_rows:
        beyond = beyond // peer_rows * padded + beyond % peer_rows
        flat = jnp.where(flat < nodes, flat, nodes + beyond)
    lists = jnp.pad(
        send_rows.reshape(n_patch, peer_rows), ((0, 0), (0, padded - peer_rows)), constant_values=-1
    )
    recv = receivers.reshape(-1)

    weights = (w_edge_in, w_edge_out, w_node_in, w_node_out)
    depths = [w.shape[0] // n_patch for w in weights]
    zs = n_patch // 2
    fused = (
        n_group == 4
        and n_patch % 4 == 0
        and width == 4 * LANES
        and all(d % PACK == 0 and 2 * d % LANES == 0 for d in depths)
    )
    own_rows = (node_tape[0], edge_tape[0], node_cot[0], edge_cot[0])
    operands = own_rows[:2] + weights + own_rows[2:]
    slots = -(-halo // LANES) * LANES
    scratch = [pltpu.VMEM(operand.shape, BF) for operand in operands]
    scratch += [
        pltpu.VMEM((edges, width), BF),
        pltpu.VMEM((nodes, width), BF),
        pltpu.SemaphoreType.DMA((len(operands),)),
        pltpu.SemaphoreType.DMA((2,)),
    ]
    for length in (edges, edges, slots):
        scratch += [pltpu.VMEM((length, 1), jnp.int32), pltpu.VMEM((1, length), jnp.int32)]
    scratch += [
        pltpu.VMEM((n_patch, padded, width), BF),
        pltpu.VMEM((n_patch, padded, width), BF),
        pltpu.VMEM((n_patch, padded, width), BF),
        pltpu.VMEM((n_patch, padded, width), BF),
        pltpu.VMEM((edges, width), BF),
        pltpu.VMEM((edges, width), BF),
        pltpu.VMEM((edges, width), F32),
        pltpu.VMEM((edges, width), BF),
        pltpu.VMEM((edges, width), F32),
        pltpu.VMEM((edges, 1), F32),
        pltpu.VMEM((edges, width), BF),
        pltpu.VMEM((nodes, width), BF),
        pltpu.VMEM((nodes, width), BF),
        pltpu.VMEM((nodes, width), BF),
        pltpu.VMEM((nodes, width), BF),
        pltpu.VMEM((nodes, width), F32),
        pltpu.VMEM((nodes, width), BF),
        pltpu.VMEM((edges, width), BF),
        pltpu.VMEM((edges, width), BF),
        pltpu.VMEM((edges, width), BF),
        pltpu.VMEM((edges, width), BF),
        pltpu.VMEM((PACK, width), F32),
    ]
    n_copies = 2 * (n_patch - 1)
    if fused:
        d_ei, d_eo, d_ni, d_no = depths
        depth_n = d_ni + d_no
        depth_o = d_eo + PACK
        piece = width // n_patch
        scratch_n = reduction_scratch(zs, depth_n, depth_n // 2 // PACK * PACK)
        scratch_e = reduction_scratch(zs, d_ei, d_ei // 2 // PACK * PACK)
        scratch_e += reduction_scratch(zs, depth_o, depth_o // 2 // PACK * PACK)
        n_copies += 3 * (9 + zs - 1)
    else:
        d_ei, d_eo, d_ni, d_no = [w.shape[0] for w in weights]
        scratch_n, scratch_e = [], []
        piece = width
    scratch += [pltpu.SemaphoreType.DMA((n_copies,)), pltpu.SemaphoreType.DMA((n_copies,))]
    scratch += scratch_n + scratch_e

    vmem = pl.BlockSpec(memory_space=pltpu.VMEM)
    anywhere = pl.BlockSpec(memory_space=pl.ANY)
    sizes = (n_group, n_patch, padded, tile, senders.shape[1], fused, factor)
    edge_grad, node_grad, p_ei, p_eo, p_ni, p_no, p_gain = pl.pallas_call(
        functools.partial(kernel, sizes),
        out_shape=[
            jax.ShapeDtypeStruct((edges, width), BF),
            jax.ShapeDtypeStruct((nodes, width), BF),
            jax.ShapeDtypeStruct((d_ei, width), F32),
            jax.ShapeDtypeStruct((d_eo, width), F32),
            jax.ShapeDtypeStruct((d_ni, width), F32),
            jax.ShapeDtypeStruct((d_no, width), F32),
            jax.ShapeDtypeStruct((PACK, piece), F32),
        ],
        in_specs=[anywhere] * 8 + [vmem] * 5 + [pl.BlockSpec(memory_space=pltpu.SMEM)],
        out_specs=[anywhere] * 2 + [vmem] * 5,
        scratch_shapes=scratch,
        compiler_params=pltpu.CompilerParams(
            collective_id=0, has_side_effects=True, vmem_limit_bytes=63 * 1024 * 1024
        ),
    )(
        *operands,
        gain_edge[None],
        gain_node[None],
        tiles_of(flat),
        tiles_of(recv),
        tiles_of(lists.reshape(-1)),
        tile_count,
    )
    if fused:
        return (edge_grad[None], node_grad[None], p_ei, p_eo, p_gain[0], p_ni, p_no, p_gain[1])

    def summed(value):
        part = lax.psum_scatter(value, "patch", scatter_dimension=0, tiled=True)
        return lax.psum(part.astype(BF), "group").astype(F32) * factor

    return (
        edge_grad[None],
        node_grad[None],
        summed(p_ei),
        summed(p_eo),
        summed(p_gain[0]),
        summed(p_ni),
        summed(p_no),
        summed(p_gain[1]),
    )


def solution(mesh):
    member = P("group", "patch", None)
    placed = (member,) * 4 + (P(),) * 6
    placed += (P("patch", None), P("patch", None), P("patch"), P("patch", None))
    rows = P("patch", None)
    return jax.shard_map(
        functools.partial(local, mesh.shape["group"], mesh.shape["patch"]),
        mesh=mesh,
        in_specs=placed,
        out_specs=(member, member, rows, rows, P("patch"), rows, rows, P("patch")),
        check_vma=False,
    )
```
